32 devices in a mesh: ctx: 8 (over z, x), head: 4 (over y, core).
Axes of the slice: x: 2, y: 2, z: 4, core: 2. Of those that a mesh axis runs over, the one named last changes fastest.
Arguments:
- query_nope: bfloat16 [256, 16384], P('head'), may hold values from -6 to 6
- query_rope: bfloat16 [256, 8192], P('head'), may hold values from -10 to 10
- latent_cache: bfloat16 [4096, 512], P('ctx'), may hold values from -6 to 6
- rope_keys: bfloat16 [64, 4096], P(None, 'ctx'), may hold values from -6 to 6
- absorb_keys: bfloat16 [128, 128, 512], P('head'), may hold values from -0.5 to 0.5
- expand_values: bfloat16 [128, 512, 128], P('head'), may hold values from -2.09375 to 2.09375
- block_ids: int32 [128, 2, 16], P('head'), may hold values from -1 to 31, as said below
- block_counts: int32 [128, 2], P('head'), may hold values from 8 to 16
Outputs:
- attended: bfloat16 [256, 16384], P('head')
The draws below stay inside these ranges and needn't reach their ends.
Inputs may be any that keep to these rules, and one draw needn't show every extreme that they name: `block_ids`: entries beyond block_counts are -1; the first block_counts entries are distinct blocks, none after the query block's own block 30 + q, and entry 0 is that own block.
All inputs are finite; a program needn't handle non-finite values.
Results may differ from the reference program's by a relative error of at most 0.0066.
Values may be sent and summed in bfloat16 or wider, within the bound.
No kernel may reach another device: no remote copies, remote signals or barrier semaphores. Data moves between devices by JAX's collectives and lax.ppermute only.
A program may use at most 128 MiB of HBM per device.

```python
import math
import jax
import jax.numpy as jnp
from jax import lax

HEADS = 128
NOPE = 128
ROPE = 64
LATENT = 512
VDIM = 128
BLOCK = 128
KSEL = 16
TOKENS = 256
CTX_DEV = 512
CONTEXT = 4096


def pick_blocks(key):
    block_total = CONTEXT // BLOCK
    query_blocks = TOKENS // BLOCK
    ranks = jax.random.randint(jax.random.fold_in(key, 4101), (HEADS, query_blocks, block_total), 0, 524288)
    ranks = ranks * block_total + jnp.arange(block_total, dtype=jnp.int32)
    own_block = block_total - query_blocks + jnp.arange(query_blocks, dtype=jnp.int32)
    later = jnp.arange(block_total, dtype=jnp.int32)[None, :] >= own_block[:, None]
    ranks = jnp.where(later[None], 1073741824 + jnp.arange(block_total, dtype=jnp.int32), ranks)
    order = jnp.argsort(ranks, axis=-1)[..., :KSEL - 1].astype(jnp.int32)
    first = jnp.broadcast_to(own_block[None, :, None], (HEADS, query_blocks, 1)).astype(jnp.int32)
    chosen = jnp.concatenate([first, order], axis=-1)
    counts = jax.random.randint(jax.random.fold_in(key, 4102), (HEADS, query_blocks), KSEL // 2, KSEL + 1)
    full_at = jax.random.randint(jax.random.fold_in(key, 4103), (), 0, HEADS * query_blocks)
    flat_index = jnp.arange(HEADS * query_blocks, dtype=jnp.int32).reshape(HEADS, query_blocks)
    counts = jnp.where(flat_index == full_at, KSEL, counts).astype(jnp.int32)
    chosen = jnp.where(jnp.arange(KSEL, dtype=jnp.int32)[None, None, :] < counts[..., None], chosen, -1)
    return (chosen.astype(jnp.int32), counts)


def draw_block_ids(key, part):
    return pick_blocks(key)[0]


def draw_block_counts(key, part):
    return pick_blocks(key)[1]


def draw_query_rope(key, part):
    values = jnp.clip(jax.random.normal(jax.random.fold_in(key, 5203), (TOKENS, HEADS * ROPE), jnp.float32), -6.0, 6.0)
    return values.astype(jnp.bfloat16)


def draw_rope_keys(key, part):
    values = jnp.clip(jax.random.normal(jax.random.fold_in(key, 5205), (ROPE, CONTEXT), jnp.float32), -6.0, 6.0)
    return values.astype(jnp.bfloat16)


def level_of(own_key, extent, pieces, least, high):
    def one(axis_at, parts):
        steps = jax.random.uniform(jax.random.fold_in(jax.random.fold_in(own_key, 6), axis_at), (parts,), jnp.float32, least / len(pieces), high / len(pieces))
        return jnp.repeat(jnp.exp(steps), extent[axis_at] // parts).reshape((-1,) + (1,) * (len(extent) - axis_at - 1))

    loudness = one(*pieces[0])
    for cut in pieces[1:]:
        loudness = loudness * one(*cut)
    return loudness


def normal_values(rng, extent, deviation, most, split=(), held_as=jnp.bfloat16):
    entries = jax.random.normal(rng, extent, jnp.float32) * deviation
    if len(split) > 0:
        entries = level_of(rng, extent, split, -0.22, 0.18) * entries
    return jnp.clip(entries, min=-most, max=most).astype(held_as)


def setup_inputs(seed: int = 0) -> dict:
    arg_keys = jax.random.split(jax.random.key(seed), 9)
    query_nope = normal_values(arg_keys[0], (TOKENS, HEADS * NOPE), 1.0, 6.0, ((0, 4),))
    query_rope = draw_query_rope(jax.random.fold_in(arg_keys[8], 71), 0)
    latent_cache = normal_values(arg_keys[2], (CONTEXT, LATENT), 1.0, 6.0, ((0, 8),))
    rope_keys = draw_rope_keys(jax.random.fold_in(arg_keys[8], 71), 0)
    absorb_keys = normal_values(arg_keys[4], (HEADS, NOPE, LATENT), NOPE ** -0.5, 0.5, ((0, 4),))
    expand_values = normal_values(arg_keys[5], (HEADS, LATENT, VDIM), 0.35, 2.09375, ((0, 4),))
    block_ids = draw_block_ids(jax.random.fold_in(arg_keys[8], 71), 0)
    block_counts = draw_block_counts(jax.random.fold_in(arg_keys[8], 71), 0)
    return {"query_nope": query_nope, "query_rope": query_rope, "latent_cache": latent_cache, "rope_keys": rope_keys, "absorb_keys": absorb_keys, "expand_values": expand_values, "block_ids": block_ids, "block_counts": block_counts}


def reference(query_nope, query_rope, latent_cache, rope_keys, absorb_keys, expand_values, block_ids, block_counts):
    tokens = query_nope.shape[0]
    heads = absorb_keys.shape[0]
    nope_width = absorb_keys.shape[1]
    latent_width = absorb_keys.shape[2]
    rope_width = rope_keys.shape[0]
    value_width = expand_values.shape[2]
    context = latent_cache.shape[0]
    block_total = context // BLOCK
    query_blocks = tokens // BLOCK
    slot_count = block_ids.shape[2]
    score_scale = 1.0 / math.sqrt(nope_width + rope_width)
    key_blocks = latent_cache.reshape(block_total, BLOCK, latent_width)
    rope_blocks = rope_keys.reshape(rope_width, block_total, BLOCK).transpose(1, 0, 2)
    nope_heads = query_nope.reshape(tokens, heads, nope_width).transpose(1, 0, 2)
    rope_heads = query_rope.reshape(tokens, heads, rope_width).transpose(1, 0, 2)
    offset = context - tokens

    def one_head(head_args):
        nope_rows, rope_rows, key_proj, value_proj, head_ids, head_counts = head_args
        query_latent = jnp.dot(nope_rows, key_proj, preferred_element_type=jnp.float32).astype(jnp.bfloat16)
        value_float = value_proj.astype(jnp.float32)

        def one_block(block_args):
            block_index, row_ids, count = block_args
            start = (block_index * BLOCK).astype(jnp.int32)
            latent_rows = lax.dynamic_slice_in_dim(query_latent, start, BLOCK, 0)
            rope_part = lax.dynamic_slice_in_dim(rope_rows, start, BLOCK, 0)
            safe_ids = jnp.maximum(row_ids, 0).astype(jnp.int32)
            keys = key_blocks[safe_ids].reshape(slot_count * BLOCK, latent_width)
            rope_cols = rope_blocks[safe_ids].transpose(1, 0, 2).reshape(rope_width, slot_count * BLOCK)
            scores = jnp.dot(latent_rows, keys.T, preferred_element_type=jnp.float32)
            scores = (scores + jnp.dot(rope_part, rope_cols, preferred_element_type=jnp.float32)) * score_scale
            query_pos = offset + start + jnp.arange(BLOCK, dtype=jnp.int32)
            key_pos = (safe_ids[:, None] * BLOCK + jnp.arange(BLOCK, dtype=jnp.int32)[None, :]).reshape(-1)
            slot_live = jnp.broadcast_to((jnp.arange(slot_count, dtype=jnp.int32) < count)[:, None], (slot_count, BLOCK)).reshape(-1)
            allowed = slot_live[None, :] & (key_pos[None, :] <= query_pos[:, None])
            masked = jnp.where(allowed, scores, -1e+30).reshape(BLOCK, slot_count, BLOCK)
            slot_max = lax.optimization_barrier(jnp.max(masked, axis=2))
            slot_segment = safe_ids * BLOCK // CTX_DEV
            same = slot_segment[:, None] == slot_segment[None, :]
            segment_top = lax.optimization_barrier(jnp.max(jnp.where(same[None], slot_max[:, None, :], -1e+30), axis=2))
            row_top = lax.optimization_barrier(jnp.max(slot_max, axis=1, keepdims=True))
            segment_cols = jnp.repeat(segment_top, BLOCK, axis=1)
            weights = jnp.where(allowed, jnp.exp(scores - segment_cols), 0.0).astype(jnp.bfloat16)
            segment_scale = jnp.exp(segment_top - row_top)
            weight_float = weights.astype(jnp.float32).reshape(BLOCK, slot_count, BLOCK)
            weight_total = lax.optimization_barrier(jnp.sum(segment_scale * lax.optimization_barrier(jnp.sum(weight_float, axis=2)), axis=1, keepdims=True))
            partial_value = jnp.einsum('rsk,skl->rsl', weight_float, keys.astype(jnp.float32).reshape(slot_count, BLOCK, latent_width), precision=lax.Precision.HIGHEST)
            latent_sum = lax.optimization_barrier(jnp.sum(segment_scale[:, :, None] * partial_value, axis=1))
            result = jnp.dot(latent_sum, value_float, precision=lax.Precision.HIGHEST) / weight_total
            return result.astype(jnp.bfloat16)
        outputs = lax.map(one_block, (jnp.arange(query_blocks, dtype=jnp.int32), head_ids, head_counts))
        return outputs.reshape(tokens, value_width)
    per_head = lax.map(one_head, (nope_heads, rope_heads, absorb_keys, expand_values, block_ids, block_counts))
    return per_head.transpose(1, 0, 2).reshape(tokens, heads * value_width)
```

```python
import functools
import math

import jax
import jax.numpy as jnp
from jax import lax
from jax.experimental import pallas as pl
from jax.experimental.pallas import tpu as pltpu
from jax.sharding import PartitionSpec as P

BLOCK = 128
NEG = -1e30


def ring_order(shards):
    across = max(d for d in range(1, shards + 1) if shards % d == 0 and d * d <= shards)
    down = shards // across
    if across == 1:
        return list(range(shards))
    walk = [z * across for z in range(down)]
    for at, z in enumerate(reversed(range(down))):
        row = [z * across + x for x in range(1, across)]
        walk += row if at % 2 == 0 else row[::-1]
    return walk


def ring_gather(block, shards):
    walk = ring_order(shards)
    ahead = [(walk[i], walk[(i + 1) % shards]) for i in range(shards)]
    back = [(dst, src) for src, dst in ahead]
    arrived = [(0, block)]
    right = left = block
    for hop in range(1, shards // 2 + 1):
        right = lax.ppermute(right, "ctx", ahead)
        arrived.append((-hop, right))
        if 2 * hop < shards:
            left = lax.ppermute(left, "ctx", back)
            arrived.append((hop, left))
    return arrived


def ring_tables(shards):
    walk = ring_order(shards)
    place = {shard: i for i, shard in enumerate(walk)}
    offsets = [0]
    for hop in range(1, shards // 2 + 1):
        offsets.append(-hop)
        if 2 * hop < shards:
            offsets.append(hop)
    source = [[walk[(place[me] + off) % shards] for off in offsets] for me in range(shards)]
    slot = [[row.index(s) for s in range(shards)] for row in source]
    return source, slot


def attend_kernel(
    shards, seg_blocks, slots, scale, heads,
    head0_ref, half_ref, slot_ref, ids_ref, counts_ref,
    q_ref, absorb_ref, expand_ref, own_ref, *rest,
):
    arrivals = rest[: 2 * (shards - 1)]
    out_ref, kv, s_ref, sems = rest[2 * (shards - 1):]
    step = pl.program_id(0)
    head = step // 2
    qblock = step % 2
    rows = seg_blocks // 2 * BLOCK
    width = kv.shape[2]
    half = half_ref[0]

    @pl.when(step == 0)
    def _():
        copies = [
            pltpu.make_async_copy(own_ref.at[half], kv.at[0], sems.at[0]),
            pltpu.make_async_copy(own_ref.at[1 - half], kv.at[shards], sems.at[1]),
        ]
        for a, ref in enumerate(arrivals):
            where = a + 1 if a < shards - 1 else a + 2
            copies.append(pltpu.make_async_copy(ref, kv.at[where], sems.at[a + 2]))
        for copy in copies:
            copy.start()
        for copy in copies:
            copy.wait()

    entry = (head0_ref[0] + head) * 2 + qblock
    count = counts_ref[entry]
    query = pl.ds(pl.multiple_of(qblock * BLOCK, BLOCK), BLOCK)
    nope = q_ref[query, pl.ds(pl.multiple_of(head * BLOCK, BLOCK), BLOCK)]
    latent = jnp.dot(nope, absorb_ref[0], preferred_element_type=jnp.float32).astype(jnp.bfloat16)
    pair = q_ref[query, pl.ds(pl.multiple_of((heads + head // 2) * BLOCK, BLOCK), BLOCK)]
    lane = lax.broadcasted_iota(jnp.int32, (BLOCK, BLOCK), 1)
    rope = jnp.where((lane >= BLOCK // 2) == (head % 2 == 1), pair, jnp.zeros_like(pair))

    def place(slot):
        block = jnp.maximum(ids_ref[entry * slots + slot], 0)
        segment = block // seg_blocks
        inside = block % seg_blocks
        at = slot_ref[segment]
        at = jnp.where(inside // (seg_blocks // 2) == half, at, at + shards)
        return at, inside % (seg_blocks // 2)

    def keys_of(slot):
        at, sub = place(slot)
        return kv[at, pl.ds(pl.multiple_of(sub * BLOCK, BLOCK), BLOCK), :]

    def rope_of(slot):
        at, sub = place(slot)
        top = kv[at, rows:, pl.ds(pl.multiple_of(sub * BLOCK, BLOCK), BLOCK)]
        low = kv[at, rows:, pl.ds(pl.multiple_of(width // 2 + sub * BLOCK, BLOCK), BLOCK)]
        return jnp.concatenate([top, low, top, low], axis=0)

    def score(group):
        keys = jnp.concatenate([keys_of(s) for s in group], axis=0)
        ropes = jnp.concatenate([rope_of(s) for s in group], axis=1)
        got = lax.dot_general(latent, keys, (((1,), (1,)), ((), ())), preferred_element_type=jnp.float32)
        got = (got + jnp.dot(rope, ropes, preferred_element_type=jnp.float32)) * scale
        parts = []
        for n, s in enumerate(group):
            part = got[:, n * BLOCK:(n + 1) * BLOCK]
            if s == 0:
                row = lax.broadcasted_iota(jnp.int32, (BLOCK, BLOCK), 0)
                part = jnp.where(lane <= row, part, NEG)
            else:
                part = jnp.where(s < count, part, NEG)
            s_ref[:, s * BLOCK:(s + 1) * BLOCK] = part
            parts.append(part)
        return functools.reduce(jnp.maximum, parts)

    tops = [score((s, s + 1)) for s in range(0, slots, 2)]
    top = jnp.max(functools.reduce(jnp.maximum, tops), axis=1, keepdims=True)
    weights = []
    sums = None
    for s in range(slots):
        w = jnp.exp(s_ref[:, s * BLOCK:(s + 1) * BLOCK] - top).astype(jnp.bfloat16)
        weights.append(w)
        wide = w.astype(jnp.float32)
        sums = wide if sums is None else sums + wide
    total = jnp.sum(sums, axis=1, keepdims=True)
    acc = jnp.dot(
        jnp.concatenate(weights, axis=1),
        jnp.concatenate([keys_of(s) for s in range(slots)], axis=0),
        preferred_element_type=jnp.float32,
    )
    high = acc.astype(jnp.bfloat16)
    low = (acc - high.astype(jnp.float32)).astype(jnp.bfloat16)
    value = jnp.dot(high, expand_ref[0], preferred_element_type=jnp.float32)
    value = value + jnp.dot(low, expand_ref[0], preferred_element_type=jnp.float32)
    out_ref[...] = (value / total).astype(jnp.bfloat16)


def place_kernel(groups, shards, where_ref, *rest):
    blocks = rest[:shards]
    out_ref, sems = rest[shards:]
    width = blocks[0].shape[2]
    copies = []
    for a, ref in enumerate(blocks):
        for g in range(groups):
            column = pl.multiple_of((g * shards + where_ref[a]) * width, width)
            copies.append(
                pltpu.make_async_copy(
                    ref.at[g], out_ref.at[:, pl.ds(column, width)], sems.at[a * groups + g]
                )
            )
    for copy in copies:
        copy.start()
    for copy in copies:
        copy.wait()


def split_body(
    query_nope, query_rope, latent_cache, rope_keys, absorb_keys, expand_values, block_ids, block_counts
):
    shards = lax.axis_size("ctx")
    groups = lax.axis_size("head")
    ctx = lax.axis_index("ctx")
    half = lax.axis_index("head") % 2
    my_tokens = query_nope.shape[0]
    tokens = my_tokens * groups
    group_heads, nope_width, latent_width = absorb_keys.shape
    rope_width, keys_here = rope_keys.shape
    value_width = expand_values.shape[2]
    slots = block_ids.shape[2]
    heads = group_heads // shards
    seg_blocks = keys_here // BLOCK
    scale = 1.0 / math.sqrt(nope_width + rope_width)
    source, slot = ring_tables(shards)
    source = jnp.array(source, jnp.int32)[ctx]
    slot = jnp.array(slot, jnp.int32)[ctx]

    half_keys = keys_here // 2
    split = latent_width // half_keys
    packs = []
    for part in range(2):
        columns = rope_keys[:, part * half_keys:(part + 1) * half_keys]
        step = rope_width // split
        columns = jnp.concatenate([columns[n * step:(n + 1) * step] for n in range(split)], axis=1)
        packs.append(
            jnp.concatenate([latent_cache[part * half_keys:(part + 1) * half_keys], columns], axis=0)
        )
    own = jnp.stack(packs)
    mine = lax.dynamic_index_in_dim(own, half, 0, keepdims=False)
    gathered = [a for _, a in ring_gather(mine, shards)][1:]
    swap = [(i, i ^ 1) for i in range(groups)]
    others = [lax.ppermute(a, "head", swap) for a in gathered]

    def for_groups(array, width):
        view = array.reshape(my_tokens, groups, group_heads * width)
        return lax.dynamic_slice_in_dim(view, ctx * heads * width, heads * width, 2)

    queries = jnp.concatenate(
        [for_groups(query_nope, nope_width), for_groups(query_rope, rope_width)], axis=2
    ).transpose(1, 0, 2)
    queries = lax.all_to_all(queries, "head", 0, 0).reshape(tokens, heads * (nope_width + rope_width))

    prefetch = (
        (ctx * heads).reshape(1).astype(jnp.int32),
        half.reshape(1).astype(jnp.int32),
        slot,
        block_ids.reshape(-1),
        block_counts.reshape(-1),
    )
    any_spec = pl.BlockSpec(memory_space=pl.ANY)
    pack_shape = mine.shape
    out = pl.pallas_call(
        functools.partial(attend_kernel, shards, seg_blocks, slots, scale, heads),
        out_shape=jax.ShapeDtypeStruct((tokens, heads * value_width), jnp.bfloat16),
        grid_spec=pltpu.PrefetchScalarGridSpec(
            num_scalar_prefetch=5,
            grid=(heads * (tokens // BLOCK),),
            in_specs=[
                pl.BlockSpec(memory_space=pltpu.VMEM),
                pl.BlockSpec((1, nope_width, latent_width), lambda i, h0, *_: (h0[0] + i // 2, 0, 0)),
                pl.BlockSpec((1, latent_width, value_width), lambda i, h0, *_: (h0[0] + i // 2, 0, 0)),
            ]
            + [any_spec] * (1 + 2 * (shards - 1)),
            out_specs=pl.BlockSpec((BLOCK, value_width), lambda i, *_: (i % 2, i // 2)),
            scratch_shapes=[
                pltpu.VMEM((2 * shards,) + pack_shape, jnp.bfloat16),
                pltpu.VMEM((BLOCK, slots * BLOCK), jnp.float32),
                pltpu.SemaphoreType.DMA((2 * shards,)),
            ],
        ),
        compiler_params=pltpu.CompilerParams(vmem_limit_bytes=32 << 20),
        name="attend",
    )(*prefetch, queries, absorb_keys, expand_values, own, *gathered, *others)

    rows = lax.all_to_all(out.reshape(groups, my_tokens, heads * value_width), "head", 0, 0)
    blocks = [a for _, a in ring_gather(rows, shards)]
    return pl.pallas_call(
        functools.partial(place_kernel, groups, shards),
        out_shape=jax.ShapeDtypeStruct((my_tokens, groups * group_heads * value_width), jnp.bfloat16),
        grid_spec=pltpu.PrefetchScalarGridSpec(
            num_scalar_prefetch=1,
            grid=(),
            in_specs=[pl.BlockSpec(memory_space=pltpu.VMEM)] * shards,
            out_specs=any_spec,
            scratch_shapes=[pltpu.SemaphoreType.DMA((shards * groups,))],
        ),
        name="place",
    )(source, *blocks)


def dense_body(
    query_nope,
    query_rope,
    latent_cache,
    rope_keys,
    absorb_keys,
    expand_values,
    block_ids,
    block_counts,
):
    nope_all, rope_all = (
        lax.all_to_all(query_nope, "head", split_axis=1, concat_axis=0, tiled=True),
        lax.all_to_all(query_rope, "head", split_axis=1, concat_axis=0, tiled=True),
    )
    tokens = nope_all.shape[0]
    heads_here = absorb_keys.shape[0]
    nope_width = absorb_keys.shape[1]
    rope_width = rope_keys.shape[0]
    value_width = expand_values.shape[2]
    keys_here = latent_cache.shape[0]
    blocks_here = keys_here // BLOCK
    query_blocks = tokens // BLOCK
    slot_count = block_ids.shape[2]
    shards = lax.axis_size("ctx")
    ctx_index = lax.axis_index("ctx")
    score_scale = 1.0 / math.sqrt(nope_width + rope_width)
    query_latent = jnp.einsum(
        "thn,hnl->htl",
        nope_all.reshape(tokens, heads_here, nope_width),
        absorb_keys,
        preferred_element_type=jnp.float32,
    ).astype(jnp.bfloat16)
    scores = jnp.einsum(
        "htl,kl->htk", query_latent, latent_cache, preferred_element_type=jnp.float32
    )
    scores = scores + jnp.einsum(
        "thr,rk->htk",
        rope_all.reshape(tokens, heads_here, rope_width),
        rope_keys,
        preferred_element_type=jnp.float32,
    )
    scores = (scores * score_scale).reshape(heads_here, query_blocks, BLOCK, blocks_here, BLOCK)
    block_global = ctx_index * blocks_here + jnp.arange(blocks_here, dtype=jnp.int32)
    slot_live = jnp.arange(slot_count, dtype=jnp.int32)[None, None, :] < block_counts[:, :, None]
    chosen = jnp.any((block_ids[..., None] == block_global) & slot_live[..., None], axis=2)
    query_pos = keys_here * shards - tokens + jnp.arange(tokens, dtype=jnp.int32)
    key_pos = ctx_index * keys_here + jnp.arange(keys_here, dtype=jnp.int32)
    causal = (key_pos[None, :] <= query_pos[:, None]).reshape(
        query_blocks, BLOCK, blocks_here, BLOCK
    )
    allowed = chosen[:, :, None, :, None] & causal[None]
    local_top = jnp.max(jnp.where(allowed, scores, -1e30), axis=(3, 4))
    weights = jnp.where(allowed, jnp.exp(scores - local_top[..., None, None]), 0.0).astype(
        jnp.bfloat16
    )
    weights = weights.reshape(heads_here, tokens, keys_here)
    top_rows = local_top.reshape(heads_here, tokens).T
    weight_total = jnp.sum(weights, axis=2, dtype=jnp.float32).T
    latent_sum = jnp.einsum(
        "htk,kl->thl", weights, latent_cache, preferred_element_type=jnp.float32
    )
    value_float = expand_values.astype(jnp.float32)
    per_device = tokens // shards
    partial_out = jnp.einsum(
        "thl,hlv->thv", latent_sum, value_float, precision=lax.Precision.HIGHEST
    )
    parts_out, parts_total, parts_top = (
        lax.all_to_all(partial_out[None], "ctx", split_axis=1, concat_axis=0, tiled=True),
        lax.all_to_all(weight_total[None], "ctx", split_axis=1, concat_axis=0, tiled=True),
        lax.all_to_all(top_rows[None], "ctx", split_axis=1, concat_axis=0, tiled=True),
    )
    best = jnp.max(parts_top, axis=0)
    factor = jnp.exp(parts_top - best[None])
    summed_out = jnp.sum(parts_out * factor[..., None], axis=0)
    summed_total = jnp.sum(parts_total * factor, axis=0)
    rows_done = (
        (summed_out / summed_total[..., None])
        .astype(jnp.bfloat16)
        .reshape(per_device, heads_here * value_width)
    )
    merged = lax.all_gather(rows_done, "ctx", axis=0, tiled=True)
    return lax.all_to_all(merged, "head", split_axis=0, concat_axis=1, tiled=True)


def body(*args):
    shards = lax.axis_size("ctx")
    groups = lax.axis_size("head")
    group_heads, nope_width, latent_width = args[4].shape
    rope_width, keys_here = args[3].shape
    gathered_bytes = 2 * shards * keys_here * (latent_width + rope_width)
    fits = (
        group_heads % (2 * shards) == 0
        and groups % 2 == 0
        and shards % 2 == 0
        and gathered_bytes <= 12 << 20
        and args[0].shape[0] * groups == 2 * BLOCK
        and nope_width == BLOCK
        and 2 * rope_width == BLOCK
        and keys_here % (2 * BLOCK) == 0
        and latent_width % (keys_here // 2) == 0
    )
    return split_body(*args) if fits else dense_body(*args)


def solution(mesh):
    return jax.shard_map(
        body,
        mesh=mesh,
        in_specs=(
            P("head", None),
            P("head", None),
            P("ctx", None),
            P(None, "ctx"),
            P("head", None, None),
            P("head", None, None),
            P("head", None, None),
            P("head", None),
        ),
        out_specs=P("head", None),
        check_vma=False,
    )
```

```python
import functools
import math

import jax
import jax.numpy as jnp
from jax import lax
from jax.experimental import pallas as pl
from jax.experimental.pallas import tpu as pltpu
from jax.sharding import PartitionSpec as P

BLOCK = 128
NEG = -1e30
ANY = pl.BlockSpec(memory_space=pl.ANY)
VMEM = pl.BlockSpec(memory_space=pltpu.VMEM)


def ring_order(shards):
    across = max(d for d in range(1, shards + 1) if shards % d == 0 and d * d <= shards)
    down = shards // across
    if across == 1:
        return list(range(shards))
    walk = [z * across for z in range(down)]
    for at, z in enumerate(reversed(range(down))):
        row = [z * across + x for x in range(1, across)]
        walk += row if at % 2 == 0 else row[::-1]
    return walk


def ring_gather(block, shards):
    walk = ring_order(shards)
    ahead = [(walk[i], walk[(i + 1) % shards]) for i in range(shards)]
    back = [(dst, src) for src, dst in ahead]
    hops = []
    right = left = block
    for hop in range(1, shards // 2 + 1):
        right = lax.ppermute(right, "ctx", ahead)
        hops.append([right])
        if 2 * hop < shards:
            left = lax.ppermute(left, "ctx", back)
            hops[-1].append(left)
    return hops


def ring_sources(shards):
    walk = ring_order(shards)
    place = {shard: i for i, shard in enumerate(walk)}
    offsets = [0]
    for hop in range(1, shards // 2 + 1):
        offsets.append(-hop)
        if 2 * hop < shards:
            offsets.append(hop)
    return [[walk[(place[me] + off) % shards] for off in offsets] for me in range(shards)]


def run_copies(pairs, sems):
    copies = [pltpu.make_async_copy(src, dst, sems.at[n]) for n, (src, dst) in enumerate(pairs)]
    for copy in copies:
        copy.start()
    for copy in copies:
        copy.wait()


def pack_pairs(latent_ref, rope_ref, out_ref, at, block):
    step = rope_ref.shape[0] * BLOCK // latent_ref.shape[1]
    keys = pl.multiple_of(block * BLOCK, BLOCK)
    pairs = [(latent_ref.at[pl.ds(keys, BLOCK), :], out_ref.at[at, pl.ds(0, BLOCK), :])]
    for n in range(rope_ref.shape[0] // step):
        pairs.append((
            rope_ref.at[pl.ds(n * step, step), pl.ds(keys, BLOCK)],
            out_ref.at[at, pl.ds(BLOCK, step), pl.ds(n * BLOCK, BLOCK)],
        ))
    return pairs


def prepare_kernel(
    groups, shards, where_ref, nope_ref, rope_q_ref, latent_ref, rope_ref,
    queries_ref, mine_ref, own_ref, sems,
):
    ctx, half = where_ref[0], where_ref[1]
    wide = nope_ref.shape[1] // (groups * shards)
    narrow = rope_q_ref.shape[1] // (groups * shards)
    pairs = []
    count = mine_ref.shape[0]
    for n in range(count):
        pairs += pack_pairs(latent_ref, rope_ref, mine_ref, n, half * count + n)
    for n in range(2 * count):
        pairs += pack_pairs(latent_ref, rope_ref, own_ref, n, n)
    for g in range(groups):
        for ref, width, at in ((nope_ref, wide, 0), (rope_q_ref, narrow, wide)):
            column = pl.multiple_of((g * shards + ctx) * width, width)
            pairs.append((ref.at[:, pl.ds(column, width)], queries_ref.at[g, :, pl.ds(at, width)]))
    run_copies(pairs, sems)


def fetch_kernel(where_ref, absorb_ref, expand_ref, absorb_out, expand_out, sems):
    heads = absorb_out.shape[0]
    first = where_ref[0] * heads
    run_copies(
        [
            (absorb_ref.at[pl.ds(first, heads)], absorb_out),
            (expand_ref.at[pl.ds(first, heads)], expand_out),
        ],
        sems,
    )


def keys_of(refs):
    return jnp.concatenate([r[n, :BLOCK, :] for r in refs for n in range(r.shape[0])], axis=0)


def ropes_of(refs):
    columns = []
    for r in refs:
        for n in range(r.shape[0]):
            rows = r[n, BLOCK:, :]
            parts = [rows[:, i * BLOCK:(i + 1) * BLOCK] for i in range(rows.shape[1] // BLOCK)]
            columns.append(jnp.concatenate(parts + parts, axis=0))
    return jnp.concatenate(columns, axis=1)


def stage_kernel(
    first, last, heads, tokens, seg_blocks, total_blocks, scale, arrays, at_arrival,
    half_ref, source_ref, reach_ref, *refs,
):
    refs = list(refs)
    head0 = heads.start
    qblocks = tokens // BLOCK
    segments = []
    for count in arrays:
        segments.append([refs.pop(0) for _ in range(count)])
    if first:
        queries_ref, absorb_ref = refs.pop(0), refs.pop(0)
        latent_out, rope_out, acc_out, top_out, sum_out = refs
    else:
        latent_in, rope_in, acc_in, top_in, sum_in = refs[:5]
        refs = refs[5:]
        if last:
            expand_ref, out_ref = refs
        else:
            acc_out, top_out, sum_out = refs
    half = half_ref[0]
    factor = scale / math.log(2.0)
    gap = lax.broadcasted_iota(jnp.int32, (BLOCK, BLOCK), 1) - lax.broadcasted_iota(
        jnp.int32, (BLOCK, BLOCK), 0
    )

    def one_head(head):
        rows = pl.ds(pl.multiple_of(head * tokens, tokens), tokens)
        if first:
            nope = queries_ref[:, pl.ds(pl.multiple_of(head * BLOCK, BLOCK), BLOCK)]
            latent = jnp.dot(nope, absorb_ref[head], preferred_element_type=jnp.float32)
            latent = latent.astype(jnp.bfloat16)
            pair = pl.multiple_of((heads.stop + head // 2) * BLOCK, BLOCK)
            pair = queries_ref[:, pl.ds(pair, BLOCK)]
            lane = lax.broadcasted_iota(jnp.int32, pair.shape, 1)
            rope = jnp.where((lane >= BLOCK // 2) == (head % 2 == 1), pair, jnp.zeros_like(pair))
            latent_out[rows, :] = latent
            rope_out[rows, :] = rope
        else:
            latent = latent_in[rows, :]
            rope = rope_in[rows, :]
        tiles = [[] for _ in range(qblocks)]
        for n, segment in enumerate(segments):
            got = lax.dot_general(
                latent, keys_of(segment), (((1,), (1,)), ((), ())), preferred_element_type=jnp.float32
            )
            got = got + jnp.dot(rope, ropes_of(segment), preferred_element_type=jnp.float32)
            base = source_ref[at_arrival + n] * seg_blocks
            for b in range(seg_blocks):
                if len(segment) == 1:
                    block = base + b
                else:
                    mine = b < seg_blocks // 2
                    part = half if mine else 1 - half
                    block = base + part * (seg_blocks // 2) + b % (seg_blocks // 2)
                for q in range(qblocks):
                    reach = reach_ref[(head * qblocks + q) * total_blocks + block]
                    tile = got[q * BLOCK:(q + 1) * BLOCK, b * BLOCK:(b + 1) * BLOCK]
                    tiles[q].append(jnp.where(gap <= reach, tile, NEG))
        weights, fades, sums = [], [], []
        for q in range(qblocks):
            top = jnp.max(functools.reduce(jnp.maximum, tiles[q]), axis=1, keepdims=True)
            at = pl.ds(pl.multiple_of(head * tokens + q * BLOCK, BLOCK), BLOCK)
            if not first:
                before = top_in[at, :]
                top = jnp.maximum(before, top)
                fade = jnp.exp2((before - top) * factor)
                fades.append(fade)
            else:
                top = jnp.broadcast_to(top, (BLOCK, BLOCK))
            mine = [jnp.exp2((t - top) * factor).astype(jnp.bfloat16) for t in tiles[q]]
            weights.append(jnp.concatenate(mine, axis=1))
            total = functools.reduce(jnp.add, [w.astype(jnp.float32) for w in mine])
            if not first:
                total = total + sum_in[at, :] * fade
            if last:
                sums.append(jnp.sum(total, axis=1, keepdims=True))
            else:
                sum_out[at, :] = total
                top_out[at, :] = top
        acc = jnp.dot(
            jnp.concatenate(weights, axis=0),
            jnp.concatenate([keys_of(segment) for segment in segments], axis=0),
            preferred_element_type=jnp.float32,
        )
        if not first:
            fade = jnp.concatenate(fades, axis=0)
            width = acc.shape[1]
            fade = jnp.concatenate([fade] * (width // BLOCK), axis=1)
            acc = acc + acc_in[rows, :] * fade
        if not last:
            acc_out[rows, :] = acc
            return
        high = acc.astype(jnp.bfloat16)
        low = (acc - high.astype(jnp.float32)).astype(jnp.bfloat16)
        value = jnp.dot(high, expand_ref[head], preferred_element_type=jnp.float32)
        value = value + jnp.dot(low, expand_ref[head], preferred_element_type=jnp.float32)
        value = (value / jnp.concatenate(sums, axis=0)).astype(jnp.bfloat16)
        out_ref[:, pl.ds(pl.multiple_of((head - head0) * BLOCK, BLOCK), BLOCK)] = value

    @pl.loop(heads.start, heads.stop)
    def _(head):
        one_head(head)


def place_kernel(groups, shards, chunks, where_ref, *rest):
    blocks = rest[:-2]
    out_ref, sems = rest[-2:]
    width = blocks[0].shape[2]
    pairs = []
    for n, ref in enumerate(blocks):
        chunk, a = divmod(n, shards)
        for g in range(groups):
            column = (g * shards + where_ref[a]) * chunks + chunk
            column = pl.multiple_of(column * width, width)
            pairs.append((ref.at[g], out_ref.at[:, pl.ds(column, width)]))
    run_copies(pairs, sems)


def split_body(
    query_nope, query_rope, latent_cache, rope_keys, absorb_keys, expand_values, block_ids, block_counts
):
    shards = lax.axis_size("ctx")
    groups = lax.axis_size("head")
    ctx = lax.axis_index("ctx")
    half = lax.axis_index("head") % 2
    my_tokens = query_nope.shape[0]
    tokens = my_tokens * groups
    group_heads, nope_width, latent_width = absorb_keys.shape
    rope_width, keys_here = rope_keys.shape
    value_width = expand_values.shape[2]
    slots = block_ids.shape[2]
    heads = group_heads // shards
    seg_blocks = keys_here // BLOCK
    total_blocks = seg_blocks * shards
    qblocks = tokens // BLOCK
    rows = heads * tokens
    scale = 1.0 / math.sqrt(nope_width + rope_width)
    source = jnp.array(ring_sources(shards), jnp.int32)[ctx]
    where = jnp.stack([ctx, half]).astype(jnp.int32)
    pack_rows = BLOCK + rope_width * BLOCK // latent_width
    bf16, f32 = jnp.bfloat16, jnp.float32

    def shape(*dims, dtype=bf16):
        return jax.ShapeDtypeStruct(dims, dtype)

    def call(kernel, name, scalars, inputs, in_specs, outs, sems=0, flops=0, aliases={}):
        return pl.pallas_call(
            kernel,
            out_shape=outs,
            grid_spec=pltpu.PrefetchScalarGridSpec(
                num_scalar_prefetch=len(scalars),
                grid=(),
                in_specs=in_specs,
                out_specs=jax.tree.map(lambda _: VMEM, outs),
                scratch_shapes=[pltpu.SemaphoreType.DMA((sems,))] if sems else [],
            ),
            input_output_aliases=aliases,
            cost_estimate=pl.CostEstimate(
                flops=flops, transcendentals=0, bytes_accessed=2 * sum(a.size for a in inputs) if flops else 1 << 20
            ),
            name=name,
        )(*scalars, *inputs)

    queries, mine, own = call(
        functools.partial(prepare_kernel, groups, shards),
        "prepare",
        (where,),
        (query_nope, query_rope, latent_cache, rope_keys),
        [ANY] * 4,
        (
            shape(groups, my_tokens, heads * (nope_width + rope_width)),
            shape(seg_blocks // 2, pack_rows, latent_width),
            shape(seg_blocks, pack_rows, latent_width),
        ),
        sems=64,
    )
    hops = ring_gather(mine, shards)
    swap = [(i, i ^ 1) for i in range(groups)]
    swapped = [[lax.ppermute(a, "head", swap) for a in hop] for hop in hops]
    queries = lax.all_to_all(queries, "head", 0, 0).reshape(tokens, heads * (nope_width + rope_width))
    absorb, expand = call(
        fetch_kernel,
        "fetch",
        (where,),
        (absorb_keys, expand_values),
        [ANY] * 2,
        (shape(heads, nope_width, latent_width), shape(heads, latent_width, value_width)),
        sems=2,
    )

    ids = lax.dynamic_slice_in_dim(block_ids, ctx * heads, heads, 0)
    counts = lax.dynamic_slice_in_dim(block_counts, ctx * heads, heads, 0)
    blocks = jnp.arange(total_blocks, dtype=jnp.int32)
    live = jnp.arange(slots, dtype=jnp.int32) < counts[..., None]
    chosen = jnp.any((ids[..., None] == blocks) & live[..., None], axis=2)
    own_block = (total_blocks - qblocks + jnp.arange(qblocks, dtype=jnp.int32))[:, None]
    reach = jnp.where(blocks == own_block, 0, BLOCK)
    reach = jnp.where(chosen & (blocks <= own_block), reach, -BLOCK).astype(jnp.int32).reshape(-1)

    scalars = (half.reshape(1).astype(jnp.int32), source, reach)
    state = [
        shape(rows, latent_width),
        shape(rows, BLOCK),
        shape(rows, latent_width, dtype=f32),
        shape(rows, BLOCK, dtype=f32),
        shape(rows, BLOCK, dtype=f32),
    ]

    def stage(first, last, span, segments, at, inputs, outs, aliases={}):
        arrays = [len(s) for s in segments]
        keys = [a for s in segments for a in s]
        share = len(span) * tokens * len(segments) * keys_here
        aliases = {len(scalars) + len(keys) + i: o for i, o in aliases.items()}
        return call(
            functools.partial(
                stage_kernel, first, last, span, tokens, seg_blocks, total_blocks, scale, arrays, at
            ),
            "attend%d_%d" % (at, span.start),
            scalars,
            tuple(keys) + tuple(inputs),
            [VMEM] * (len(keys) + len(inputs)),
            outs,
            flops=2 * share * (2 * latent_width + rope_width),
            aliases=aliases,
        )

    arrived = [[[a, b] for a, b in zip(hop, other)] for hop, other in zip(hops, swapped)]
    segments = [[own]] + arrived[0]
    latent, rope, *running = stage(
        True, False, range(heads), segments, 0, (queries, absorb), tuple(state)
    )
    at = len(segments)
    for segments in arrived[1:-1]:
        running = stage(
            False, False, range(heads), segments, at, (latent, rope, *running), tuple(state[2:]),
            aliases={2: 0, 3: 1, 4: 2},
        )
        at += len(segments)
    pieces = []
    chunks = 2
    for n in range(chunks):
        span = range(n * heads // chunks, (n + 1) * heads // chunks)
        out = stage(
            False, True, span, arrived[-1], at, (latent, rope, *running, expand),
            shape(tokens, len(span) * value_width),
        )
        out = lax.all_to_all(out.reshape(groups, my_tokens, len(span) * value_width), "head", 0, 0)
        pieces += [out] + [a for hop in ring_gather(out, shards) for a in hop]
    return pl.pallas_call(
        functools.partial(place_kernel, groups, shards, chunks),
        out_shape=shape(my_tokens, groups * group_heads * value_width),
        grid_spec=pltpu.PrefetchScalarGridSpec(
            num_scalar_prefetch=1,
            grid=(),
            in_specs=[VMEM] * len(pieces),
            out_specs=ANY,
            scratch_shapes=[pltpu.SemaphoreType.DMA((len(pieces) * groups,))],
        ),
        name="place",
    )(source, *pieces)


def dense_body(
    query_nope,
    query_rope,
    latent_cache,
    rope_keys,
    absorb_keys,
    expand_values,
    block_ids,
    block_counts,
):
    nope_all, rope_all = (
        lax.all_to_all(query_nope, "head", split_axis=1, concat_axis=0, tiled=True),
        lax.all_to_all(query_rope, "head", split_axis=1, concat_axis=0, tiled=True),
    )
    tokens = nope_all.shape[0]
    heads_here = absorb_keys.shape[0]
    nope_width = absorb_keys.shape[1]
    rope_width = rope_keys.shape[0]
    value_width = expand_values.shape[2]
    keys_here = latent_cache.shape[0]
    blocks_here = keys_here // BLOCK
    query_blocks = tokens // BLOCK
    slot_count = block_ids.shape[2]
    shards = lax.axis_size("ctx")
    ctx_index = lax.axis_index("ctx")
    score_scale = 1.0 / math.sqrt(nope_width + rope_width)
    query_latent = jnp.einsum(
        "thn,hnl->htl",
        nope_all.reshape(tokens, heads_here, nope_width),
        absorb_keys,
        preferred_element_type=jnp.float32,
    ).astype(jnp.bfloat16)
    scores = jnp.einsum(
        "htl,kl->htk", query_latent, latent_cache, preferred_element_type=jnp.float32
    )
    scores = scores + jnp.einsum(
        "thr,rk->htk",
        rope_all.reshape(tokens, heads_here, rope_width),
        rope_keys,
        preferred_element_type=jnp.float32,
    )
    scores = (scores * score_scale).reshape(heads_here, query_blocks, BLOCK, blocks_here, BLOCK)
    block_global = ctx_index * blocks_here + jnp.arange(blocks_here, dtype=jnp.int32)
    slot_live = jnp.arange(slot_count, dtype=jnp.int32)[None, None, :] < block_counts[:, :, None]
    chosen = jnp.any((block_ids[..., None] == block_global) & slot_live[..., None], axis=2)
    query_pos = keys_here * shards - tokens + jnp.arange(tokens, dtype=jnp.int32)
    key_pos = ctx_index * keys_here + jnp.arange(keys_here, dtype=jnp.int32)
    causal = (key_pos[None, :] <= query_pos[:, None]).reshape(
        query_blocks, BLOCK, blocks_here, BLOCK
    )
    allowed = chosen[:, :, None, :, None] & causal[None]
    local_top = jnp.max(jnp.where(allowed, scores, -1e30), axis=(3, 4))
    weights = jnp.where(allowed, jnp.exp(scores - local_top[..., None, None]), 0.0).astype(
        jnp.bfloat16
    )
    weights = weights.reshape(heads_here, tokens, keys_here)
    top_rows = local_top.reshape(heads_here, tokens).T
    weight_total = jnp.sum(weights, axis=2, dtype=jnp.float32).T
    latent_sum = jnp.einsum(
        "htk,kl->thl", weights, latent_cache, preferred_element_type=jnp.float32
    )
    value_float = expand_values.astype(jnp.float32)
    per_device = tokens // shards
    partial_out = jnp.einsum(
        "thl,hlv->thv", latent_sum, value_float, precision=lax.Precision.HIGHEST
    )
    parts_out, parts_total, parts_top = (
        lax.all_to_all(partial_out[None], "ctx", split_axis=1, concat_axis=0, tiled=True),
        lax.all_to_all(weight_total[None], "ctx", split_axis=1, concat_axis=0, tiled=True),
        lax.all_to_all(top_rows[None], "ctx", split_axis=1, concat_axis=0, tiled=True),
    )
    best = jnp.max(parts_top, axis=0)
    factor = jnp.exp(parts_top - best[None])
    summed_out = jnp.sum(parts_out * factor[..., None], axis=0)
    summed_total = jnp.sum(parts_total * factor, axis=0)
    rows_done = (
        (summed_out / summed_total[..., None])
        .astype(jnp.bfloat16)
        .reshape(per_device, heads_here * value_width)
    )
    merged = lax.all_gather(rows_done, "ctx", axis=0, tiled=True)
    return lax.all_to_all(merged, "head", split_axis=0, concat_axis=1, tiled=True)


def body(*args):
    shards = lax.axis_size("ctx")
    groups = lax.axis_size("head")
    group_heads, nope_width, latent_width = args[4].shape
    rope_width, keys_here = args[3].shape
    gathered_bytes = 2 * shards * keys_here * (latent_width + rope_width)
    fits = (
        group_heads % (4 * shards) == 0
        and groups % 2 == 0
        and shards % 2 == 0
        and shards >= 4
        and gathered_bytes <= 12 << 20
        and args[0].shape[0] * groups % BLOCK == 0
        and nope_width == BLOCK
        and 2 * rope_width == BLOCK
        and args[5].shape[2] == BLOCK
        and keys_here % (2 * BLOCK) == 0
        and latent_width % BLOCK == 0
        and rope_width * BLOCK % (16 * latent_width) == 0
    )
    return split_body(*args) if fits else dense_body(*args)


def solution(mesh):
    return jax.shard_map(
        body,
        mesh=mesh,
        in_specs=(
            P("head", None),
            P("head", None),
            P("ctx", None),
            P(None, "ctx"),
            P("head", None, None),
            P("head", None, None),
            P("head", None, None),
            P("head", None),
        ),
        out_specs=P("head", None),
        check_vma=False,
    )
```

```python
import functools
import math

import jax
import jax.numpy as jnp
from jax import lax
from jax.experimental import pallas as pl
from jax.experimental.pallas import tpu as pltpu
from jax.sharding import PartitionSpec as P

BLOCK = 128
NEG = -1e30
CHUNKS = 2
HBM = pl.BlockSpec(memory_space=pltpu.HBM)
SMEM = pl.BlockSpec(memory_space=pltpu.SMEM)
VMEM = pl.BlockSpec(memory_space=pltpu.VMEM)


def ring_order(shards):
    across = max(d for d in range(1, shards + 1) if shards % d == 0 and d * d <= shards)
    down = shards // across
    if across == 1:
        return list(range(shards))
    walk = [z * across for z in range(down)]
    for at, z in enumerate(reversed(range(down))):
        row = [z * across + x for x in range(1, across)]
        walk += row if at % 2 == 0 else row[::-1]
    return walk


def ring_gather(block, shards):
    walk = ring_order(shards)
    ahead = [(walk[i], walk[(i + 1) % shards]) for i in range(shards)]
    back = [(dst, src) for src, dst in ahead]
    hops = []
    right = left = block
    for hop in range(1, shards // 2 + 1):
        right = lax.ppermute(right, "ctx", ahead)
        hops.append([right])
        if 2 * hop < shards:
            left = lax.ppermute(left, "ctx", back)
            hops[-1].append(left)
    return hops


def ring_offsets(shards):
    offsets = [0]
    for hop in range(1, shards // 2 + 1):
        offsets.append(-hop)
        if 2 * hop < shards:
            offsets.append(hop)
    return offsets


def lookup(table, index):
    found = jnp.int32(table[0])
    for n, entry in enumerate(table[1:], 1):
        found = jnp.where(index == n, entry, found)
    return found


def ring_source(shards, arrival):
    walk = ring_order(shards)
    place = [walk.index(shard) for shard in range(shards)]
    at = lookup(place, lax.axis_index("ctx")) + ring_offsets(shards)[arrival] + shards
    return lookup(walk, lax.rem(at, shards))


def run_copies(pairs, sems):
    copies = [pltpu.make_async_copy(src, dst, sems.at[n]) for n, (src, dst) in enumerate(pairs)]
    for copy in copies:
        copy.start()
    for copy in copies:
        copy.wait()


def pack_pairs(latent_ref, rope_ref, out_ref, at, block):
    step = rope_ref.shape[0] * BLOCK // latent_ref.shape[1]
    keys = pl.multiple_of(block * BLOCK, BLOCK)
    pairs = [(latent_ref.at[pl.ds(keys, BLOCK), :], out_ref.at[at, pl.ds(0, BLOCK), :])]
    for n in range(rope_ref.shape[0] // step):
        pairs.append((
            rope_ref.at[pl.ds(n * step, step), pl.ds(keys, BLOCK)],
            out_ref.at[at, pl.ds(BLOCK, step), pl.ds(n * BLOCK, BLOCK)],
        ))
    return pairs


def mine_kernel(latent_ref, rope_ref, mine_ref, sems):
    half = lax.rem(lax.axis_index("head"), 2)
    count = mine_ref.shape[0]
    pairs = []
    for n in range(count):
        pairs += pack_pairs(latent_ref, rope_ref, mine_ref, n, half * count + n)
    run_copies(pairs, sems)


def queries_kernel(groups, shards, nope_ref, rope_q_ref, latent_ref, rope_ref, *rest):
    queries, own_ref, sems = rest[:groups], rest[groups], rest[groups + 1]
    ctx, group = lax.axis_index("ctx"), lax.axis_index("head")
    wide = nope_ref.shape[1] // (groups * shards)
    narrow = rope_q_ref.shape[1] // (groups * shards)
    pairs = []
    for d in reversed(range(groups)):
        for ref, width, at in ((nope_ref, wide, 0), (rope_q_ref, narrow, wide)):
            column = pl.multiple_of((lax.bitwise_xor(group, d) * shards + ctx) * width, width)
            pairs.append((ref.at[:, pl.ds(column, width)], queries[d].at[:, pl.ds(at, width)]))
    for n in range(own_ref.shape[0]):
        pairs += pack_pairs(latent_ref, rope_ref, own_ref, n, n)
    run_copies(pairs, sems)


def fetch_kernel(total_blocks, ids_ref, counts_ref, absorb_ref, expand_ref, absorb_out, expand_out, reach_ref, sems):
    heads = absorb_out.shape[0]
    first = lax.axis_index("ctx") * heads
    copies = [
        pltpu.make_async_copy(absorb_ref.at[pl.ds(first, heads)], absorb_out, sems.at[0]),
        pltpu.make_async_copy(expand_ref.at[pl.ds(first, heads)], expand_out, sems.at[1]),
    ]
    for copy in copies:
        copy.start()
    qblocks, slots = ids_ref.shape[:2]

    @pl.loop(0, heads * qblocks * total_blocks)
    def _(n):
        reach_ref[n] = -BLOCK

    @pl.loop(0, heads * qblocks)
    def _(row):
        head = first + row // qblocks
        q = lax.rem(row, qblocks)
        own_block = total_blocks - qblocks + q

        @pl.loop(0, counts_ref[q, head])
        def _(slot):
            block = ids_ref[q, slot, head]
            reach = jnp.where(block == own_block, 0, jnp.where(block < own_block, BLOCK, -BLOCK))
            reach_ref[row * total_blocks + block] = reach

    for copy in copies:
        copy.wait()


def merge_kernel(*refs):
    for n, ref in enumerate(refs[:-1]):
        refs[-1][n] = ref[...]


def keys_of(refs):
    return jnp.concatenate([r[n, :BLOCK, :] for r in refs for n in range(r.shape[0])], axis=0)


def ropes_of(refs):
    columns = []
    for r in refs:
        for n in range(r.shape[0]):
            rows = r[n, BLOCK:, :]
            parts = [rows[:, i * BLOCK:(i + 1) * BLOCK] for i in range(rows.shape[1] // BLOCK)]
            columns.append(jnp.concatenate(parts + parts, axis=0))
    return jnp.concatenate(columns, axis=1)


def stage_kernel(
    first, last, heads, tokens, groups, shards, seg_blocks, scale, arrays, at_arrival, reach_ref, *refs,
):
    refs = list(refs)
    head0 = heads.start
    qblocks = tokens // BLOCK
    segments = []
    for count in arrays:
        segments.append([refs.pop(0) for _ in range(count)])
    if first:
        parts, absorb_ref = refs[:groups], refs[groups]
        latent_out, rope_out, acc_out, top_out, sum_out, queries_ref = refs[groups + 1:]
        for d, part in enumerate(parts):
            at = lax.bitwise_xor(lax.axis_index("head"), d) * part.shape[0]
            queries_ref[pl.ds(pl.multiple_of(at, part.shape[0]), part.shape[0]), :] = part[...]
    else:
        latent_in, rope_in, acc_in, top_in, sum_in = refs[:5]
        refs = refs[5:]
        if last:
            expand_ref, outs, out_ref = refs[0], refs[1:-1], refs[-1]
        else:
            acc_out, top_out, sum_out = refs
    half = lax.rem(lax.axis_index("head"), 2)
    total_blocks = seg_blocks * shards
    factor = scale / math.log(2.0)
    gap = lax.broadcasted_iota(jnp.int32, (BLOCK, BLOCK), 1) - lax.broadcasted_iota(
        jnp.int32, (BLOCK, BLOCK), 0
    )

    def one_head(head):
        rows = pl.ds(pl.multiple_of(head * tokens, tokens), tokens)
        if first:
            nope = queries_ref[:, pl.ds(pl.multiple_of(head * BLOCK, BLOCK), BLOCK)]
            latent = jnp.dot(nope, absorb_ref[head], preferred_element_type=jnp.float32)
            latent = latent.astype(jnp.bfloat16)
            pair = pl.multiple_of((heads.stop + head // 2) * BLOCK, BLOCK)
            pair = queries_ref[:, pl.ds(pair, BLOCK)]
            lane = lax.broadcasted_iota(jnp.int32, pair.shape, 1)
            rope = jnp.where((lane >= BLOCK // 2) == (head % 2 == 1), pair, jnp.zeros_like(pair))
            latent_out[rows, :] = latent
            rope_out[rows, :] = rope
        else:
            latent = latent_in[rows, :]
            rope = rope_in[rows, :]
        tiles = [[] for _ in range(qblocks)]
        for n, segment in enumerate(segments):
            got = lax.dot_general(
                latent, keys_of(segment), (((1,), (1,)), ((), ())), preferred_element_type=jnp.float32
            )
            got = got + jnp.dot(rope, ropes_of(segment), preferred_element_type=jnp.float32)
            base = ring_source(shards, at_arrival + n) * seg_blocks
            for b in range(seg_blocks):
                if len(segment) == 1:
                    block = base + b
                else:
                    mine = b < seg_blocks // 2
                    part = half if mine else 1 - half
                    block = base + part * (seg_blocks // 2) + b % (seg_blocks // 2)
                for q in range(qblocks):
                    reach = reach_ref[(head * qblocks + q) * total_blocks + block]
                    tile = got[q * BLOCK:(q + 1) * BLOCK, b * BLOCK:(b + 1) * BLOCK]
                    tiles[q].append(jnp.where(gap <= reach, tile, NEG))
        weights, fades, sums = [], [], []
        for q in range(qblocks):
            top = jnp.max(functools.reduce(jnp.maximum, tiles[q]), axis=1, keepdims=True)
            at = pl.ds(pl.multiple_of(head * tokens + q * BLOCK, BLOCK), BLOCK)
            if not first:
                before = top_in[at, :]
                top = jnp.maximum(before, top)
                fade = jnp.exp2((before - top) * factor)
                fades.append(fade)
            else:
                top = jnp.broadcast_to(top, (BLOCK, BLOCK))
            mine = [jnp.exp2((t - top) * factor).astype(jnp.bfloat16) for t in tiles[q]]
            weights.append(jnp.concatenate(mine, axis=1))
            total = functools.reduce(jnp.add, [w.astype(jnp.float32) for w in mine])
            if not first:
                total = total + sum_in[at, :] * fade
            if last:
                sums.append(jnp.sum(total, axis=1, keepdims=True))
            else:
                sum_out[at, :] = total
                top_out[at, :] = top
        acc = jnp.dot(
            jnp.concatenate(weights, axis=0),
            jnp.concatenate([keys_of(segment) for segment in segments], axis=0),
            preferred_element_type=jnp.float32,
        )
        if not first:
            fade = jnp.concatenate(fades, axis=0)
            width = acc.shape[1]
            fade = jnp.concatenate([fade] * (width // BLOCK), axis=1)
            acc = acc + acc_in[rows, :] * fade
        if not last:
            acc_out[rows, :] = acc
            return
        high = acc.astype(jnp.bfloat16)
        low = (acc - high.astype(jnp.float32)).astype(jnp.bfloat16)
        value = jnp.dot(high, expand_ref[head], preferred_element_type=jnp.float32)
        value = value + jnp.dot(low, expand_ref[head], preferred_element_type=jnp.float32)
        value = (value / jnp.concatenate(sums, axis=0)).astype(jnp.bfloat16)
        out_ref[:, pl.ds(pl.multiple_of((head - head0) * BLOCK, BLOCK), BLOCK)] = value

    @pl.loop(heads.start, heads.stop)
    def _(head):
        one_head(head)

    if last:
        for d, ref in enumerate(outs):
            at = lax.bitwise_xor(lax.axis_index("head"), d) * ref.shape[0]
            ref[...] = out_ref[pl.ds(pl.multiple_of(at, ref.shape[0]), ref.shape[0]), :]


def place_kernel(groups, shards, chunks, *rest):
    blocks = rest[:-2]
    out_ref, sems = rest[-2:]
    group = lax.axis_index("head")
    width = blocks[0].shape[2]
    pairs = []
    for n, ref in enumerate(blocks):
        chunk, arrival = divmod(n, shards)
        source = ring_source(shards, arrival)
        for d in range(groups):
            column = ((lax.bitwise_xor(group, d)) * shards + source) * chunks + chunk
            column = pl.multiple_of(column * width, width)
            pairs.append((ref.at[d], out_ref.at[:, pl.ds(column, width)]))
    run_copies(pairs, sems)


def split_body(
    query_nope, query_rope, latent_cache, rope_keys, absorb_keys, expand_values, block_ids, block_counts
):
    shards = lax.axis_size("ctx")
    groups = lax.axis_size("head")
    my_tokens = query_nope.shape[0]
    tokens = my_tokens * groups
    group_heads, nope_width, latent_width = absorb_keys.shape
    rope_width, keys_here = rope_keys.shape
    value_width = expand_values.shape[2]
    heads = group_heads // shards
    seg_blocks = keys_here // BLOCK
    total_blocks = seg_blocks * shards
    qblocks = tokens // BLOCK
    rows = heads * tokens
    query_width = heads * (nope_width + rope_width)
    scale = 1.0 / math.sqrt(nope_width + rope_width)
    pack_rows = BLOCK + rope_width * BLOCK // latent_width
    i32, bf16, f32 = jnp.int32, jnp.bfloat16, jnp.float32

    def call(kernel, name, inputs, outs, scratch=(), sems=0, flops=0, aliases={}, scalars=()):
        operands = [
            pltpu.with_memory_space_constraint(a, spec.memory_space) if spec is not SMEM else a
            for a, spec in inputs
        ]
        return pl.pallas_call(
            kernel,
            out_shape=outs,
            grid_spec=pltpu.PrefetchScalarGridSpec(
                num_scalar_prefetch=len(scalars),
                grid=(),
                in_specs=[spec for _, spec in inputs],
                out_specs=jax.tree.map(lambda o: pl.BlockSpec(memory_space=o.memory_space), outs),
                scratch_shapes=list(scratch) + ([pltpu.SemaphoreType.DMA((sems,))] if sems else []),
            ),
            input_output_aliases=aliases,
            cost_estimate=pl.CostEstimate(flops=flops, transcendentals=0, bytes_accessed=4 << 20),
            compiler_params=pltpu.CompilerParams(vmem_limit_bytes=8 << 20),
            name=name,
        )(*scalars, *operands)

    swap = [(i, i ^ 1) for i in range(groups)]

    def exchange(parts):
        moved = [
            lax.ppermute(part, "head", [(i, i ^ d) for i in range(groups)])
            for d, part in reversed(list(enumerate(parts))[1:])
        ]
        return [parts[0]] + moved[::-1]

    mine = call(
        mine_kernel, "mine", [(latent_cache, HBM), (rope_keys, HBM)],
        pltpu.VMEM((seg_blocks // 2, pack_rows, latent_width), bf16), sems=32,
    )
    *queries, own = call(
        functools.partial(queries_kernel, groups, shards), "queries",
        [(query_nope, HBM), (query_rope, HBM), (latent_cache, HBM), (rope_keys, HBM)],
        (pltpu.VMEM((my_tokens, query_width), bf16),) * groups
        + (pltpu.VMEM((seg_blocks, pack_rows, latent_width), bf16),),
        sems=64,
    )
    queries = exchange(queries)
    absorb, expand, reach = call(
        functools.partial(fetch_kernel, total_blocks), "fetch",
        [(block_ids.transpose(1, 2, 0), SMEM), (block_counts.T, SMEM), (absorb_keys, HBM), (expand_values, HBM)],
        (
            pltpu.VMEM((heads, nope_width, latent_width), bf16),
            pltpu.VMEM((heads, latent_width, value_width), bf16),
            pltpu.SMEM((heads * qblocks * total_blocks,), i32),
        ),
        sems=2,
    )
    state = (
        pltpu.VMEM((rows, latent_width), bf16),
        pltpu.VMEM((rows, BLOCK), bf16),
        pltpu.VMEM((rows, latent_width), f32),
        pltpu.VMEM((rows, BLOCK), f32),
        pltpu.VMEM((rows, BLOCK), f32),
    )

    def stage(first, last, span, segments, at, inputs, outs, scratch=(), aliases={}):
        arrays = [len(s) for s in segments]
        keys = [a for s in segments for a in s]
        share = len(span) * tokens * len(segments) * keys_here
        return call(
            functools.partial(
                stage_kernel, first, last, span, tokens, groups, shards, seg_blocks, scale, arrays, at
            ),
            "attend%d_%d" % (at, span.start),
            [(a, VMEM) for a in keys + list(inputs)],
            outs,
            scratch=scratch,
            flops=2 * share * (2 * latent_width + rope_width),
            aliases={1 + len(keys) + i: o for i, o in aliases.items()},
            scalars=(reach,),
        )

    walk = ring_order(shards)
    ahead = [(walk[i], walk[(i + 1) % shards]) for i in range(shards)]
    back = [(dst, src) for src, dst in ahead]
    hops = shards // 2
    everyone = range(heads)
    fresh = [lax.ppermute(mine, "ctx", ahead), lax.ppermute(mine, "ctx", back)]
    segments, at, running = [[own]], 0, None
    for hop in range(1, hops + 1):
        following = []
        if hop < hops:
            following.append(lax.ppermute(fresh[0], "ctx", ahead))
            if 2 * (hop + 1) < shards:
                following.append(lax.ppermute(fresh[1], "ctx", back))
        segments += [[a, lax.ppermute(a, "head", swap)] for a in fresh]
        if hop == hops:
            break
        if running is None:
            latent, rope, *running = stage(
                True, False, everyone, segments, at, (*queries, absorb), state,
                scratch=[pltpu.VMEM((tokens, query_width), bf16)],
            )
        else:
            running = stage(
                False, False, everyone, segments, at, (latent, rope, *running), state[2:],
                aliases={2: 0, 3: 1, 4: 2},
            )
        at += len(segments)
        segments = []
        fresh, running = lax.optimization_barrier((following, running))
    pieces = []
    for n in range(CHUNKS):
        span = range(n * heads // CHUNKS, (n + 1) * heads // CHUNKS)
        width = len(span) * value_width
        outs = stage(
            False, True, span, segments, at, (latent, rope, *running, expand),
            (pltpu.VMEM((my_tokens, width), bf16),) * groups,
            scratch=[pltpu.VMEM((tokens, width), bf16)],
        )
        merged = call(
            merge_kernel, "merge%d" % n, [(a, VMEM) for a in exchange(outs)],
            pltpu.VMEM((groups, my_tokens, width), bf16),
        )
        pieces += [merged] + [a for hop in ring_gather(merged, shards) for a in hop]
    return call(
        functools.partial(place_kernel, groups, shards, CHUNKS), "place",
        [(a, VMEM) for a in pieces],
        pltpu.HBM((my_tokens, groups * group_heads * value_width), bf16),
        sems=len(pieces) * groups,
    )

def dense_body(
    query_nope,
    query_rope,
    latent_cache,
    rope_keys,
    absorb_keys,
    expand_values,
    block_ids,
    block_counts,
):
    nope_all, rope_all = (
        lax.all_to_all(query_nope, "head", split_axis=1, concat_axis=0, tiled=True),
        lax.all_to_all(query_rope, "head", split_axis=1, concat_axis=0, tiled=True),
    )
    tokens = nope_all.shape[0]
    heads_here = absorb_keys.shape[0]
    nope_width = absorb_keys.shape[1]
    rope_width = rope_keys.shape[0]
    value_width = expand_values.shape[2]
    keys_here = latent_cache.shape[0]
    blocks_here = keys_here // BLOCK
    query_blocks = tokens // BLOCK
    slot_count = block_ids.shape[2]
    shards = lax.axis_size("ctx")
    ctx_index = lax.axis_index("ctx")
    score_scale = 1.0 / math.sqrt(nope_width + rope_width)
    query_latent = jnp.einsum(
        "thn,hnl->htl",
        nope_all.reshape(tokens, heads_here, nope_width),
        absorb_keys,
        preferred_element_type=jnp.float32,
    ).astype(jnp.bfloat16)
    scores = jnp.einsum(
        "htl,kl->htk", query_latent, latent_cache, preferred_element_type=jnp.float32
    )
    scores = scores + jnp.einsum(
        "thr,rk->htk",
        rope_all.reshape(tokens, heads_here, rope_width),
        rope_keys,
        preferred_element_type=jnp.float32,
    )
    scores = (scores * score_scale).reshape(heads_here, query_blocks, BLOCK, blocks_here, BLOCK)
    block_global = ctx_index * blocks_here + jnp.arange(blocks_here, dtype=jnp.int32)
    slot_live = jnp.arange(slot_count, dtype=jnp.int32)[None, None, :] < block_counts[:, :, None]
    chosen = jnp.any((block_ids[..., None] == block_global) & slot_live[..., None], axis=2)
    query_pos = keys_here * shards - tokens + jnp.arange(tokens, dtype=jnp.int32)
    key_pos = ctx_index * keys_here + jnp.arange(keys_here, dtype=jnp.int32)
    causal = (key_pos[None, :] <= query_pos[:, None]).reshape(
        query_blocks, BLOCK, blocks_here, BLOCK
    )
    allowed = chosen[:, :, None, :, None] & causal[None]
    local_top = jnp.max(jnp.where(allowed, scores, -1e30), axis=(3, 4))
    weights = jnp.where(allowed, jnp.exp(scores - local_top[..., None, None]), 0.0).astype(
        jnp.bfloat16
    )
    weights = weights.reshape(heads_here, tokens, keys_here)
    top_rows = local_top.reshape(heads_here, tokens).T
    weight_total = jnp.sum(weights, axis=2, dtype=jnp.float32).T
    latent_sum = jnp.einsum(
        "htk,kl->thl", weights, latent_cache, preferred_element_type=jnp.float32
    )
    value_float = expand_values.astype(jnp.float32)
    per_device = tokens // shards
    partial_out = jnp.einsum(
        "thl,hlv->thv", latent_sum, value_float, precision=lax.Precision.HIGHEST
    )
    parts_out, parts_total, parts_top = (
        lax.all_to_all(partial_out[None], "ctx", split_axis=1, concat_axis=0, tiled=True),
        lax.all_to_all(weight_total[None], "ctx", split_axis=1, concat_axis=0, tiled=True),
        lax.all_to_all(top_rows[None], "ctx", split_axis=1, concat_axis=0, tiled=True),
    )
    best = jnp.max(parts_top, axis=0)
    factor = jnp.exp(parts_top - best[None])
    summed_out = jnp.sum(parts_out * factor[..., None], axis=0)
    summed_total = jnp.sum(parts_total * factor, axis=0)
    rows_done = (
        (summed_out / summed_total[..., None])
        .astype(jnp.bfloat16)
        .reshape(per_device, heads_here * value_width)
    )
    merged = lax.all_gather(rows_done, "ctx", axis=0, tiled=True)
    return lax.all_to_all(merged, "head", split_axis=0, concat_axis=1, tiled=True)


def body(*args):
    shards = lax.axis_size("ctx")
    groups = lax.axis_size("head")
    group_heads, nope_width, latent_width = args[4].shape
    rope_width, keys_here = args[3].shape
    gathered_bytes = 2 * shards * keys_here * (latent_width + rope_width)
    fits = (
        group_heads % (2 * CHUNKS * shards) == 0
        and groups > 1
        and groups & (groups - 1) == 0
        and shards % 2 == 0
        and shards >= 4
        and gathered_bytes <= 12 << 20
        and args[0].shape[0] * groups % BLOCK == 0
        and nope_width == BLOCK
        and 2 * rope_width == BLOCK
        and args[5].shape[2] == BLOCK
        and keys_here % (2 * BLOCK) == 0
        and latent_width % BLOCK == 0
        and rope_width * BLOCK % (16 * latent_width) == 0
    )
    return split_body(*args) if fits else dense_body(*args)


def solution(mesh):
    return jax.shard_map(
        body,
        mesh=mesh,
        in_specs=(
            P("head", None),
            P("head", None),
            P("ctx", None),
            P(None, "ctx"),
            P("head", None, None),
            P("head", None, None),
            P("head", None, None),
            P("head", None),
        ),
        out_specs=P("head", None),
        check_vma=False,
    )
```
